32 devices in a mesh: parts: 2 (over y), slab: 4 (over z), orb: 2 (over x), pen: 2 (over core).
Axes of the slice: x: 2, y: 2, z: 4, core: 2. Of those that a mesh axis runs over, the one named last changes fastest.
Arguments:
- orbitals: float32 [128, 16, 8, 256], P(('parts', 'orb'), 'slab', 'pen'), parts along dimension 0, may hold values from -7.6 to 7.6
- energies: float32 [128], P(('parts', 'orb')), parts along dimension 0, may hold values from -1 to 0.5
- frequency: float32 [2], P('parts'), parts along dimension 0, may hold values from 0.5 to 2
- local_potential: float32 [16, 8, 256], P('slab', 'pen'), may hold values from -1 to 1
- perturbation: float32 [16, 8, 256], P('slab', 'pen'), may hold values from 0.5 to 1.5
- projectors: float32 [128, 8, 256], P(None, 'pen'), may hold values from -0.0625 to 0.0625
- profiles: float32 [128, 5], replicated, may hold values from 0.5 to 2
- couplings: float32 [128], replicated, may hold values from 4 to 12
- atom_planes: int32 [128], replicated, may hold values from 0 to 15
Outputs:
- response_real: float32 [128, 16, 8, 256], P(('parts', 'orb'), 'slab', 'pen'), parts along dimension 0
- density: float32 [32, 8, 256], P(('parts', 'slab'), 'pen'), parts along dimension 0
The draws below stay inside these ranges and needn't reach their ends.
There are 2 independent parts, one for each index of `parts`. The reference program is written for one: setup_inputs(seed, part) draws one part's arguments, and reference() takes and returns one part's arrays. A program takes and returns all parts, laid end to end along the dimension named above; an argument that names none is the same for every part. Nothing has to cross between parts.
Inputs may be any that keep to these rules, and one draw needn't show every extreme that they name: Projector a covers the planes (atom_planes[a] + d) mod 16 of the first dimension for d < 5.
All inputs are finite; a program needn't handle non-finite values.
Results may differ from the reference program's by a relative error of at most 0.0003.
Values sent between devices are 32-bit elements; how exact they have to be, the bound alone decides.
A program may use at most 64 MiB of HBM per device.

```python
import math
import jax
import jax.numpy as jnp
from jax import lax

NOCC = 64
NPROJ = 128
PSPAN = 5
ITERS = 2
NX = 256
NZ = 16
NY = 8
NCELL = 32768


def draw_orbitals(key, part):
    key_own = jax.random.fold_in(key, 11)
    key_common = jax.random.fold_in(key, 12)
    key_mix = jax.random.fold_in(key, 13)
    own_part = jnp.clip(jax.random.normal(key_own, (NOCC, NZ, NY, NX), jnp.float32), -4.0, 4.0)
    common_part = jnp.clip(jax.random.normal(key_common, (NZ, NY, NX), jnp.float32), -4.0, 4.0)
    mixing = jax.random.uniform(key_mix, (NOCC,), jnp.float32, 0.3, 0.7)
    return own_part + mixing[:, None, None, None] * common_part[None]


def potential_field(key):
    key_size = jax.random.fold_in(key, 21)
    key_sign = jax.random.fold_in(key, 22)
    magnitude = jax.random.uniform(key_size, (NZ, NY, NX), jnp.float32, 0.3, 1.0)
    signs = jnp.where(jax.random.bernoulli(key_sign, 0.5, (NZ, NY, NX)), 1.0, -1.0).astype(jnp.float32)
    return magnitude * signs


def draw_local_potential(key, part):
    return potential_field(key)


def draw_perturbation(key, part):
    potential = potential_field(key)
    noise = jax.random.uniform(jax.random.fold_in(key, 23), (NZ, NY, NX), jnp.float32, -1.0, 1.0)
    return jnp.clip(1.0 + 0.5 * potential + 0.04 * noise, 0.5, 1.5)


def with_ends(entries, key, smallest, largest):
    dims = entries.shape
    index_at = [jax.random.randint(jax.random.fold_in(key, axis), (), 0, dims[axis]) for axis in range(len(dims))]
    entries = entries.at[tuple(index_at)].set(smallest)
    longest = dims.index(max(dims))
    index_at[longest] = (index_at[longest] + 1) % dims[longest]
    return entries.at[tuple(index_at)].set(largest)


def level_of(own_key, shape, cuts, smallest, high):
    factor_of, own = 1.0, jax.random.fold_in(own_key, 6)
    for position, blocks in cuts:
        steps = jnp.exp(jax.random.uniform(jax.random.fold_in(own, position), (blocks,), jnp.float32, smallest / len(cuts), high / len(cuts)))
        factor_of = factor_of * jnp.repeat(steps, shape[position] // blocks).reshape([-1 if axis == position else 1 for axis in range(len(shape))])
    return factor_of


def gaussian(rng, extent, scale, most, shards=(), kind=jnp.bfloat16):
    drawn = jax.random.normal(rng, extent, jnp.float32) * scale
    if len(shards) > 0:
        drawn = level_of(rng, extent, shards, -0.22, 0.18) * drawn
    return jnp.clip(drawn, min=-most, max=most).astype(kind)


def setup_inputs(seed: int = 0, part: int = 0) -> dict:
    key_list = jax.random.split(jax.random.key(seed), 10)
    part_keys = jax.random.split(jax.random.fold_in(key_list[9], part), 10)
    orbitals = draw_orbitals(jax.random.fold_in(jax.random.fold_in(key_list[9], part), 71), part)
    energies = jnp.clip(-1.0 + 1.5 * jax.random.uniform(part_keys[1], (NOCC,), jnp.float32) ** level_of(part_keys[1], (NOCC,), ((0, 2),), -0.2, 0.2), -1.0, 0.5)
    frequency = jnp.clip(jnp.exp(jax.random.uniform(part_keys[2], (1,), jnp.float32, math.log(0.5), math.log(2.0))), 0.5, 2.0)
    local_potential = draw_local_potential(jax.random.fold_in(key_list[9], 71), part)
    perturbation = draw_perturbation(jax.random.fold_in(key_list[9], 71), part)
    projectors = gaussian(key_list[5], (NPROJ, NY, NX), (PSPAN * NY * NX) ** -0.5, 0.0625, ((1, 2),), jnp.float32)
    profiles = jnp.clip(jax.random.uniform(key_list[6], (NPROJ, PSPAN), jnp.float32, 0.5, 2.0), 0.5, 2.0)
    couplings = jnp.clip(jax.random.uniform(key_list[7], (NPROJ,), jnp.float32, 4.0, 12.0), 4.0, 12.0)
    atom_planes = with_ends(jax.random.randint(key_list[8], (NPROJ,), 0, NZ), jax.random.fold_in(key_list[8], 1), 0, NZ - 1).astype(jnp.int32)
    return {"orbitals": orbitals, "energies": energies, "frequency": frequency, "local_potential": local_potential, "perturbation": perturbation, "projectors": projectors, "profiles": profiles, "couplings": couplings, "atom_planes": atom_planes}


kinetic_scale = 0.125
highest = lax.Precision.HIGHEST

def kinetic(values):
    beside_all = jnp.roll(values, 1, 1) + jnp.roll(values, -1, 1)
    beside_all = beside_all + jnp.roll(values, 1, 2) + jnp.roll(values, -1, 2)
    beside_all = beside_all + jnp.roll(values, 1, 3) + jnp.roll(values, -1, 3)
    return kinetic_scale * (6.0 * values - beside_all)

def plane_weights(atom_planes, profiles, planes):
    span_size = profiles.shape[1]
    covered = (atom_planes[:, None] + jnp.arange(span_size, dtype=jnp.int32)[None, :]) % NZ
    matches = (covered[:, :, None] == planes[None, None, :]).astype(jnp.float32)
    return jnp.sum(profiles[:, :, None] * matches, axis=1)

def shifted(values, local_potential, projectors, weights, couplings, energies):
    inner_sums = jnp.einsum('ayx,izyx->aiz', projectors, values, precision=highest)
    expansion = couplings[:, None] * jnp.einsum('aiz,az->ai', inner_sums, weights, precision=highest)
    spread = weights[:, None, :] * expansion[:, :, None]
    nonlocal_term = jnp.einsum('aiz,ayx->izyx', spread, projectors, precision=highest)
    return kinetic(values) + local_potential[None] * values + nonlocal_term - energies[:, None, None, None] * values

def remove(values, orbitals, factor):
    correlation = jnp.einsum('jzyx,izyx->ji', orbitals, values, precision=highest) / NCELL
    expansion = jax.scipy.linalg.cho_solve((factor, True), correlation)
    return values - jnp.einsum('ji,jzyx->izyx', expansion, orbitals, precision=highest)

def reference(orbitals, energies, frequency, local_potential, perturbation, projectors, profiles, couplings, atom_planes):
    weights = plane_weights(atom_planes, profiles, jnp.arange(NZ, dtype=jnp.int32))
    gram = jnp.einsum('jzyx,kzyx->jk', orbitals, orbitals, precision=highest) / NCELL
    factor = jnp.linalg.cholesky(gram)
    freq_square = frequency[0] * frequency[0]

    def apply_shift(values):
        return shifted(values, local_potential, projectors, weights, couplings, energies)
    residual = -remove(perturbation[None] * orbitals, orbitals, factor)
    direction = residual
    solution = jnp.zeros_like(residual)
    norm_now = jnp.sum(residual * residual, axis=(1, 2, 3))
    for iteration in range(ITERS):
        inner_field = remove(direction, orbitals, factor)
        first_half = apply_shift(inner_field)
        image_field = remove(apply_shift(first_half) + freq_square * inner_field, orbitals, factor)
        step_size = norm_now / jnp.sum(direction * image_field, axis=(1, 2, 3))
        solution = solution + step_size[:, None, None, None] * direction
        residual = residual - step_size[:, None, None, None] * image_field
        norm_next = jnp.sum(residual * residual, axis=(1, 2, 3))
        direction = residual + (norm_next / norm_now)[:, None, None, None] * direction
        norm_now = norm_next
    response_real = apply_shift(solution)
    density = 4.0 / NOCC * jnp.sum(orbitals * response_real, axis=0)
    return (response_real, density)
```

```python
import functools

import jax
import jax.numpy as jnp
from jax import lax
from jax.experimental import pallas as pl
from jax.experimental.pallas import tpu as pltpu
from jax.sharding import PartitionSpec as P

kinetic_scale = 0.125
MESH = pl.DeviceIdType.MESH
f32, bf16 = jnp.float32, jnp.bfloat16
NT = (((1,), (1,)), ((), ()))
NN = (((1,), (0,)), ((), ()))


def split(x):
    hi = x.astype(bf16)
    return hi, (x - hi.astype(f32)).astype(bf16)


def dot3(a, b, dims):
    rows = a[0].shape[0]
    both = lax.dot_general(jnp.concatenate(a, axis=0), b[0], dims, preferred_element_type=f32)
    rest = lax.dot_general(a[0], b[1], dims, preferred_element_type=f32)
    return both[:rows] + both[rows:] + rest


def inverse(a):
    size = a.shape[0]
    row_id = lax.broadcasted_iota(jnp.int32, (size, size), 0)
    col_id = lax.broadcasted_iota(jnp.int32, (size, size), 1)
    one_row = lax.broadcasted_iota(jnp.int32, (1, size), 1)
    for k in range(size):
        inv = 1.0 / a[k : k + 1, k : k + 1]
        column = a[:, k : k + 1]
        row = jnp.where(one_row == k, inv, a[k : k + 1, :] * inv)
        updated = jnp.where(col_id == k, 0.0, a) - column * row
        a = jnp.where(row_id == k, row, updated)
    return a


def kernel(
    slabs, pens, orbs, orb_ref, en_ref, freq_ref, vloc_ref, dv_ref, beta_ref, table_ref, coup_ref,
    resp_ref, dens_ref,
    others, phi_hi, phi_lo, u_hi, u_lo, pad0, pad1, pad2, work, dens_slots,
    gram_slots, red_slots,
    gather_send, gather_recv, halo_send, halo_recv, red_send, red_recv, dens_send, dens_recv,
):
    planes, rows, count, width = orb_ref.shape
    atoms = beta_ref.shape[1]
    span = table_ref.shape[1] - 1
    total_orbs = count * orbs
    depth = planes * slabs
    cells = float(depth * rows * pens * width)
    slab, pen, orb = lax.axis_index("slab"), lax.axis_index("pen"), lax.axis_index("orb")
    group = slabs * pens
    me = slab * pens + pen

    def peer(k):
        target = lax.rem(me + k, group)
        return {"slab": target // pens, "pen": lax.rem(target, pens)}

    barrier = pltpu.get_barrier_semaphore()
    for k in range(1, group):
        pl.semaphore_signal(barrier, inc=1, device_id=peer(k), device_id_type=MESH)
    for k in range(1, orbs):
        pl.semaphore_signal(
            barrier, inc=1, device_id={"orb": lax.rem(orb + k, orbs)}, device_id_type=MESH
        )
    pl.semaphore_wait(barrier, group - 1 + orbs - 1)

    sent = []

    def start(src, dst, send, recv, device):
        copy = pltpu.make_async_remote_copy(
            src_ref=src, dst_ref=dst, send_sem=send, recv_sem=recv,
            device_id=device, device_id_type=MESH,
        )
        copy.start()
        sent.append(copy)
        return copy

    gathers = [
        start(orb_ref, others.at[k - 1], gather_send.at[k - 1], gather_recv.at[k - 1],
              {"orb": lax.rem(orb + k, orbs)})
        for k in range(1, orbs)
    ]

    def halo_start(pad, index):
        up, down = lax.rem(slab + 1, slabs), lax.rem(slab + slabs - 1, slabs)
        right, left = lax.rem(pen + 1, pens), lax.rem(pen + pens - 1, pens)
        inner_p, inner_r = pl.ds(1, planes), pl.ds(1, rows)
        sides = (
            (pad.at[planes, inner_r], pad.at[0, inner_r], {"slab": up}),
            (pad.at[1, inner_r], pad.at[planes + 1, inner_r], {"slab": down}),
            (pad.at[inner_p, rows], pad.at[inner_p, 0], {"pen": right}),
            (pad.at[inner_p, 1], pad.at[inner_p, rows + 1], {"pen": left}),
        )
        return [
            start(src, dst, halo_send.at[index, side], halo_recv.at[index, side], device)
            for side, (src, dst, device) in enumerate(sides)
        ]

    def reduce_start(slots, index, values):
        slots[me] = values
        return [
            start(slots.at[me], slots.at[me], red_send.at[index, k - 1], red_recv.at[index, k - 1],
                  peer(k))
            for k in range(1, group)
        ]

    def reduce_end(slots, copies, index):
        for k in range(1, group):
            source = lax.rem(me + group - k, group)
            pltpu.make_async_remote_copy(
                src_ref=slots.at[source], dst_ref=slots.at[source],
                send_sem=red_send.at[index, k - 1], recv_sem=red_recv.at[index, k - 1],
                device_id=peer(k), device_id_type=MESH,
            ).wait_recv()
        total = slots[0]
        for k in range(1, group):
            total = total + slots[k]
        return total

    atom = table_ref[:, span : span + 1]
    for z in range(planes):
        plane = (slab * planes + z).astype(f32)
        weight = jnp.zeros((atoms, 1), f32)
        for d in range(span):
            covered = atom + float(d)
            covered = jnp.where(covered >= float(depth), covered - float(depth), covered)
            weight = weight + jnp.where(covered == plane, table_ref[:, d : d + 1], 0.0)
        for y in range(rows):
            hi, lo = split(beta_ref[y] * weight)
            u_hi[z, y] = hi
            u_lo[z, y] = lo

    for copy in gathers:
        copy.wait_recv()

    def put_phi(z, carry):
        for y in range(rows):
            for k in range(orbs):
                hi, lo = split(orb_ref[z, y] if k == 0 else others[k - 1, z, y])
                phi_hi[z, y, k * count : (k + 1) * count] = hi
                phi_lo[z, y, k * count : (k + 1) * count] = lo
        return carry

    lax.fori_loop(0, planes, put_phi, 0)

    def phi(z, y):
        return phi_hi[z, y], phi_lo[z, y]

    def u(z, y):
        return u_hi[z, y], u_lo[z, y]

    def gram_part(z, acc):
        for y in range(rows):
            source = dv_ref[z, pl.ds(y, 1), :] * orb_ref[z, y]
            s_hi, s_lo = split(source)
            left = (
                jnp.concatenate([phi_hi[z, y], s_hi], axis=0),
                jnp.concatenate([phi_lo[z, y], s_lo], axis=0),
            )
            acc = acc + dot3(left, phi(z, y), NT)
        return acc

    part = lax.fori_loop(0, planes, gram_part, jnp.zeros((total_orbs + count, total_orbs), f32))
    half = (total_orbs + count) // 2
    packed = jnp.concatenate([part[:half], part[half:]], axis=1)
    copies = reduce_start(gram_slots, 0, packed)
    packed = reduce_end(gram_slots, copies, 0) * (1.0 / cells)
    full = jnp.concatenate([packed[:, :total_orbs], packed[:, total_orbs:]], axis=0)
    gram_inverse = split(inverse(full[:total_orbs]))

    def solve(correlation):
        return split(dot3(split(correlation), gram_inverse, NN))

    zero_field = jnp.zeros((count, width), f32)
    zero_inner = jnp.zeros((count, atoms), f32)
    energy = en_ref[...]
    coupling = coup_ref[...]
    freq_square = freq_ref[0] * freq_ref[0]

    g = solve(full[total_orbs:])

    def first_residual(z, carry):
        inner, norm = carry
        for y in range(rows):
            source = dv_ref[z, pl.ds(y, 1), :] * orb_ref[z, y]
            r = dot3(g, phi(z, y), NN) - source
            pad0[z + 1, y + 1] = r
            inner = inner + dot3(split(r), u(z, y), NT)
            norm = norm + r * r
        return inner, norm

    inner, norm = lax.fori_loop(0, planes, first_residual, (zero_inner, zero_field))
    halos = halo_start(pad0, 0)
    copies = reduce_start(red_slots.at[0], 1, inner)
    norm0_part = jnp.sum(norm, axis=1, keepdims=True)

    def shifted(pad, coefficients, z, y):
        centre = pad[z + 1, y + 1]
        beside = pad[z, y + 1] + pad[z + 2, y + 1] + pad[z + 1, y] + pad[z + 1, y + 2]
        beside = beside + pltpu.roll(centre, 1, 1) + pltpu.roll(centre, width - 1, 1)
        diagonal = (6.0 * kinetic_scale + vloc_ref[z, pl.ds(y, 1), :]) - energy
        return diagonal * centre - kinetic_scale * beside + dot3(coefficients, u(z, y), NN)

    inner = reduce_end(red_slots.at[0], copies, 1)
    coefficients0 = split(inner * coupling)
    for copy in halos:
        copy.wait_recv()

    def first_apply(z, carry):
        inner, norm = carry
        for y in range(rows):
            first = shifted(pad0, coefficients0, z, y)
            pad1[z + 1, y + 1] = first
            inner = inner + dot3(split(first), u(z, y), NT)
            norm = norm + first * first
        return inner, norm

    inner, norm = lax.fori_loop(0, planes, first_apply, (zero_inner, zero_field))
    halos = halo_start(pad1, 1)
    copies = reduce_start(red_slots.at[1], 2, inner)
    first0_part = jnp.sum(norm, axis=1, keepdims=True)
    inner = reduce_end(red_slots.at[1], copies, 2)
    coefficients1 = split(inner * coupling)
    for copy in halos:
        copy.wait_recv()

    def second_apply(z, correlation):
        for y in range(rows):
            target = shifted(pad1, coefficients1, z, y) + freq_square * pad0[z + 1, y + 1]
            work[z, y] = target
            correlation = correlation + dot3(split(target), phi(z, y), NT)
        return correlation

    correlation = lax.fori_loop(
        0, planes, second_apply, jnp.zeros((count, total_orbs), f32)
    )
    lane = lax.broadcasted_iota(jnp.int32, (count, atoms), 1)

    def scalars(parts):
        out = jnp.zeros((count, atoms), f32)
        for k, part in enumerate(parts):
            out = jnp.where(lane == k, part, out)
        return out

    tail = scalars((norm0_part, first0_part))[:, : red_slots.shape[3] - total_orbs]
    copies = reduce_start(red_slots.at[2], 3, jnp.concatenate([correlation, tail], axis=1))
    total = reduce_end(red_slots.at[2], copies, 3)
    norm0 = total[:, total_orbs : total_orbs + 1]
    first0 = total[:, total_orbs + 1 : total_orbs + 2]
    step0 = norm0 / (first0 + freq_square * norm0)
    g = solve(total[:, :total_orbs] * (1.0 / cells))

    def second_residual(z, carry):
        inner, norm, cross = carry
        for y in range(rows):
            before = pad0[z + 1, y + 1]
            image = work[z, y] - dot3(g, phi(z, y), NN)
            r = before - step0 * image
            pad2[z + 1, y + 1] = r
            inner = inner + dot3(split(r), u(z, y), NT)
            norm = norm + r * r
            cross = cross + r * before
        return inner, norm, cross

    inner, norm, cross = lax.fori_loop(
        0, planes, second_residual, (zero_inner, zero_field, zero_field)
    )
    halos = halo_start(pad2, 2)
    copies = reduce_start(red_slots.at[3], 4, inner)
    norm1_part = jnp.sum(norm, axis=1, keepdims=True)
    cross_part = jnp.sum(cross, axis=1, keepdims=True)
    inner = reduce_end(red_slots.at[3], copies, 4)
    coefficients2 = split(inner * coupling)
    for copy in halos:
        copy.wait_recv()

    def third_apply(z, carry):
        square, cross = carry
        for y in range(rows):
            first = shifted(pad2, coefficients2, z, y)
            work[z, y] = first
            square = square + first * first
            cross = cross + first * pad1[z + 1, y + 1]
        return square, cross

    square, cross = lax.fori_loop(0, planes, third_apply, (zero_field, zero_field))
    square_part = jnp.sum(square, axis=1, keepdims=True)
    mixed_part = jnp.sum(cross, axis=1, keepdims=True)
    copies = reduce_start(
        red_slots.at[4], 5, scalars((norm1_part, cross_part, square_part, mixed_part))
    )
    total = reduce_end(red_slots.at[4], copies, 5)
    norm1, cross, square, mixed = (total[:, k : k + 1] for k in range(4))
    ratio = norm1 / norm0
    curvature = (
        square + 2.0 * ratio * mixed + ratio * ratio * first0
        + freq_square * (norm1 + 2.0 * ratio * cross + ratio * ratio * norm0)
    )
    step1 = norm1 / curvature
    scale0 = step0 + step1 * ratio

    def finish(z, carry):
        for y in range(rows):
            response = scale0 * pad1[z + 1, y + 1] + step1 * work[z, y]
            resp_ref[z, y] = response
            dens_slots[0, z, pl.ds(y, 1), :] = jnp.sum(
                orb_ref[z, y] * response, axis=0, keepdims=True
            )
        return carry

    lax.fori_loop(0, planes, finish, 0)
    last = [
        start(dens_slots.at[0], dens_slots.at[k], dens_send.at[k - 1], dens_recv.at[k - 1],
              {"orb": lax.rem(orb + k, orbs)})
        for k in range(1, orbs)
    ]
    for copy in last:
        copy.wait_recv()
    density = dens_slots[0]
    for k in range(1, orbs):
        density = density + dens_slots[k]
    dens_ref[...] = density * (4.0 / total_orbs)
    for copy in sent:
        copy.wait_send()


def solution(mesh):
    slabs, pens, orbs = mesh.shape["slab"], mesh.shape["pen"], mesh.shape["orb"]

    def on_device(
        orbitals, energies, frequency, local_potential, perturbation, projectors, profiles,
        couplings, atom_planes,
    ):
        count, planes, rows, width = orbitals.shape
        atoms = projectors.shape[0]
        total_orbs, group = count * orbs, slabs * pens
        table = jnp.concatenate([profiles, atom_planes[:, None].astype(f32)], axis=1)
        vmem = pl.BlockSpec(memory_space=pltpu.VMEM)
        smem = pl.BlockSpec(memory_space=pltpu.SMEM)
        dma = pltpu.SemaphoreType.DMA
        response, density = pl.pallas_call(
            functools.partial(kernel, slabs, pens, orbs),
            out_shape=(
                jax.ShapeDtypeStruct((planes, rows, count, width), f32),
                jax.ShapeDtypeStruct((planes, rows, width), f32),
            ),
            in_specs=[vmem, vmem, smem, vmem, vmem, vmem, vmem, vmem],
            out_specs=(vmem, vmem),
            scratch_shapes=[
                pltpu.VMEM((orbs - 1, planes, rows, count, width), f32),
                pltpu.VMEM((planes, rows, total_orbs, width), bf16),
                pltpu.VMEM((planes, rows, total_orbs, width), bf16),
                pltpu.VMEM((planes, rows, atoms, width), bf16),
                pltpu.VMEM((planes, rows, atoms, width), bf16),
                pltpu.VMEM((planes + 2, rows + 2, count, width), f32),
                pltpu.VMEM((planes + 2, rows + 2, count, width), f32),
                pltpu.VMEM((planes + 2, rows + 2, count, width), f32),
                pltpu.VMEM((planes, rows, count, width), f32),
                pltpu.VMEM((orbs, planes, rows, width), f32),
                pltpu.VMEM((group, (total_orbs + count) // 2, 2 * total_orbs), f32),
                pltpu.VMEM((5, group, count, atoms), f32),
                dma((orbs - 1,)), dma((orbs - 1,)),
                dma((3, 4)), dma((3, 4)),
                dma((6, group - 1)), dma((6, group - 1)),
                dma((orbs - 1,)), dma((orbs - 1,)),
            ],
            compiler_params=pltpu.CompilerParams(collective_id=0, has_side_effects=True),
        )(
            jnp.transpose(orbitals, (1, 2, 0, 3)),
            energies[:, None],
            frequency,
            local_potential,
            perturbation,
            jnp.transpose(projectors, (1, 0, 2)),
            table,
            couplings[None, :],
        )
        return jnp.transpose(response, (2, 0, 1, 3)), density

    in_specs = (
        P(("parts", "orb"), "slab", "pen", None), P(("parts", "orb")), P("parts"),
        P("slab", "pen", None), P("slab", "pen", None), P(None, "pen", None), P(), P(), P(),
    )
    out_specs = (P(("parts", "orb"), "slab", "pen", None), P(("parts", "slab"), "pen", None))
    return jax.shard_map(
        on_device, mesh=mesh, in_specs=in_specs, out_specs=out_specs, check_vma=False
    )
```

```python
import functools

import jax
import jax.numpy as jnp
from jax import lax
from jax.experimental import pallas as pl
from jax.experimental.pallas import tpu as pltpu
from jax.sharding import PartitionSpec as P

kinetic_scale = 0.125
MESH = pl.DeviceIdType.MESH
f32, bf16 = jnp.float32, jnp.bfloat16
NT = (((1,), (1,)), ((), ()))
NN = (((1,), (0,)), ((), ()))


def split(x):
    hi = x.astype(bf16)
    return hi, (x - hi.astype(f32)).astype(bf16)


def dot3(a, b, dims):
    rows = a[0].shape[0]
    both = lax.dot_general(jnp.concatenate(a, axis=0), b[0], dims, preferred_element_type=f32)
    rest = lax.dot_general(a[0], b[1], dims, preferred_element_type=f32)
    return both[:rows] + both[rows:] + rest


def inverse(a):
    size = a.shape[0]
    row_id = lax.broadcasted_iota(jnp.int32, (size, size), 0)
    col_id = lax.broadcasted_iota(jnp.int32, (size, size), 1)
    one_row = lax.broadcasted_iota(jnp.int32, (1, size), 1)
    for k in range(size):
        inv = 1.0 / a[k : k + 1, k : k + 1]
        column = a[:, k : k + 1]
        row = jnp.where(one_row == k, inv, a[k : k + 1, :] * inv)
        updated = jnp.where(col_id == k, 0.0, a) - column * row
        a = jnp.where(row_id == k, row, updated)
    return a


def kernel(
    slabs, pens, orbs, orb_ref, en_ref, freq_ref, vloc_ref, dv_ref, beta_ref, table_ref, coup_ref,
    resp_ref, dens_ref,
    others, phz, phz_hi, phz_lo, dvz, tz, phi_hi, phi_lo, u_hi, u_lo, pad0, pad1, pad2, work, dens_slots,
    gram_slots, red_slots,
    gather_send, gather_recv, plane_send, plane_recv, halo_send, halo_recv, red_send, red_recv, dens_send, dens_recv,
):
    planes, rows, count, width = orb_ref.shape
    atoms = beta_ref.shape[1]
    span = table_ref.shape[1] - 1
    total_orbs = count * orbs
    depth = planes * slabs
    cells = float(depth * rows * pens * width)
    slab, pen, orb = lax.axis_index("slab"), lax.axis_index("pen"), lax.axis_index("orb")
    group = slabs * pens
    me = slab * pens + pen

    def peer(k):
        target = lax.rem(me + k, group)
        return {"slab": target // pens, "pen": lax.rem(target, pens)}

    barrier = pltpu.get_barrier_semaphore()
    for k in range(1, group):
        pl.semaphore_signal(barrier, inc=1, device_id=peer(k), device_id_type=MESH)
    for k in range(1, orbs):
        pl.semaphore_signal(
            barrier, inc=1, device_id={"orb": lax.rem(orb + k, orbs)}, device_id_type=MESH
        )
    pl.semaphore_wait(barrier, group - 1 + orbs - 1)

    sent = []

    def start(src, dst, send, recv, device):
        copy = pltpu.make_async_remote_copy(
            src_ref=src, dst_ref=dst, send_sem=send, recv_sem=recv,
            device_id=device, device_id_type=MESH,
        )
        copy.start()
        sent.append(copy)
        return copy

    pieces = [pl.ds(0, 1), pl.ds(planes - 1, 1)]
    if planes > 2:
        pieces.append(pl.ds(1, planes - 2))
    gathers = [
        [
            start(orb_ref.at[piece], others.at[k - 1, piece], gather_send.at[k - 1, n],
                  gather_recv.at[k - 1, n], {"orb": lax.rem(orb + k, orbs)})
            for k in range(1, orbs)
        ]
        for n, piece in enumerate(pieces)
    ]

    up, down = lax.rem(slab + 1, slabs), lax.rem(slab + slabs - 1, slabs)

    def plane_start(low, high, below, above, index):
        return [
            start(low, above, plane_send.at[index, 0], plane_recv.at[index, 0], {"slab": down}),
            start(high, below, plane_send.at[index, 1], plane_recv.at[index, 1], {"slab": up}),
        ]

    beside = plane_start(
        dv_ref.at[0], dv_ref.at[planes - 1], dvz.at[0], dvz.at[1], orbs
    ) + plane_start(
        orb_ref.at[0], orb_ref.at[planes - 1], phz.at[0, 0], phz.at[1, 0], 0
    )

    def halo_start(pad, index, wanted):
        right, left = lax.rem(pen + 1, pens), lax.rem(pen + pens - 1, pens)
        inner_p, inner_r = pl.ds(1, planes), pl.ds(1, rows)
        sides = (
            (pad.at[planes, inner_r], pad.at[0, inner_r], {"slab": up}),
            (pad.at[1, inner_r], pad.at[planes + 1, inner_r], {"slab": down}),
            (pad.at[inner_p, rows], pad.at[inner_p, 0], {"pen": right}),
            (pad.at[inner_p, 1], pad.at[inner_p, rows + 1], {"pen": left}),
        )
        return [
            start(src, dst, halo_send.at[index, side], halo_recv.at[index, side], device)
            for side, (src, dst, device) in enumerate(sides)
            if side in wanted
        ]

    def reduce_start(slots, index, values):
        slots[me] = values
        return [
            start(slots.at[me], slots.at[me], red_send.at[index, k - 1], red_recv.at[index, k - 1],
                  peer(k))
            for k in range(1, group)
        ]

    def reduce_end(slots, copies, index):
        for k in range(1, group):
            source = lax.rem(me + group - k, group)
            pltpu.make_async_remote_copy(
                src_ref=slots.at[source], dst_ref=slots.at[source],
                send_sem=red_send.at[index, k - 1], recv_sem=red_recv.at[index, k - 1],
                device_id=peer(k), device_id_type=MESH,
            ).wait_recv()
        total = slots[0]
        for k in range(1, group):
            total = total + slots[k]
        return total

    atom = table_ref[:, span : span + 1]
    for z in range(planes):
        plane = (slab * planes + z).astype(f32)
        weight = jnp.zeros((atoms, 1), f32)
        for d in range(span):
            covered = atom + float(d)
            covered = jnp.where(covered >= float(depth), covered - float(depth), covered)
            weight = weight + jnp.where(covered == plane, table_ref[:, d : d + 1], 0.0)
        for y in range(rows):
            hi, lo = split(beta_ref[y] * weight)
            u_hi[z, y] = hi
            u_lo[z, y] = lo

    for piece in gathers[:2]:
        for copy in piece:
            copy.wait_recv()
    for k in range(1, orbs):
        beside += plane_start(
            others.at[k - 1, 0], others.at[k - 1, planes - 1], phz.at[0, k], phz.at[1, k], k
        )
    for piece in gathers[2:]:
        for copy in piece:
            copy.wait_recv()

    def put_phi(z, carry):
        for y in range(rows):
            for k in range(orbs):
                hi, lo = split(orb_ref[z, y] if k == 0 else others[k - 1, z, y])
                phi_hi[z, y, k * count : (k + 1) * count] = hi
                phi_lo[z, y, k * count : (k + 1) * count] = lo
        return carry

    lax.fori_loop(0, planes, put_phi, 0)

    def phi(z, y):
        return phi_hi[z, y], phi_lo[z, y]

    def u(z, y):
        return u_hi[z, y], u_lo[z, y]

    def gram_part(z, acc):
        for y in range(rows):
            source = dv_ref[z, pl.ds(y, 1), :] * orb_ref[z, y]
            s_hi, s_lo = split(source)
            left = (
                jnp.concatenate([phi_hi[z, y], s_hi], axis=0),
                jnp.concatenate([phi_lo[z, y], s_lo], axis=0),
            )
            acc = acc + dot3(left, phi(z, y), NT)
        return acc

    part = lax.fori_loop(0, planes, gram_part, jnp.zeros((total_orbs + count, total_orbs), f32))
    half = (total_orbs + count) // 2
    packed = jnp.concatenate([part[:half], part[half:]], axis=1)
    copies = reduce_start(gram_slots, 0, packed)
    packed = reduce_end(gram_slots, copies, 0) * (1.0 / cells)
    full = jnp.concatenate([packed[:, :total_orbs], packed[:, total_orbs:]], axis=0)
    gram_inverse = split(inverse(full[:total_orbs]))

    def solve(correlation):
        return split(dot3(split(correlation), gram_inverse, NN))

    zero_field = jnp.zeros((count, width), f32)
    zero_inner = jnp.zeros((count, atoms), f32)
    energy = en_ref[...]
    coupling = coup_ref[...]
    freq_square = freq_ref[0] * freq_ref[0]

    g = solve(full[total_orbs:])

    def first_residual(z, carry):
        inner, norm = carry
        for y in range(rows):
            source = dv_ref[z, pl.ds(y, 1), :] * orb_ref[z, y]
            r = dot3(g, phi(z, y), NN) - source
            pad0[z + 1, y + 1] = r
            inner = inner + dot3(split(r), u(z, y), NT)
            norm = norm + r * r
        return inner, norm

    inner, norm = lax.fori_loop(0, planes, first_residual, (zero_inner, zero_field))
    halos = halo_start(pad0, 0, (2, 3))
    copies = reduce_start(red_slots.at[0], 1, inner)
    norm0_part = jnp.sum(norm, axis=1, keepdims=True)
    for copy in beside:
        copy.wait_recv()

    def phi_beside(side, y):
        return phz_hi[side, y], phz_lo[side, y]

    for side, at in ((0, 0), (1, planes + 1)):
        for y in range(rows):
            for k in range(orbs):
                hi, lo = split(phz[side, k, y])
                phz_hi[side, y, k * count : (k + 1) * count] = hi
                phz_lo[side, y, k * count : (k + 1) * count] = lo
            source = dvz[side, y : y + 1, :] * phz[side, 0, y]
            pad0[at, y + 1] = dot3(g, phi_beside(side, y), NN) - source

    def shifted(pad, coefficients, z, y):
        centre = pad[z + 1, y + 1]
        beside = pad[z, y + 1] + pad[z + 2, y + 1] + pad[z + 1, y] + pad[z + 1, y + 2]
        beside = beside + pltpu.roll(centre, 1, 1) + pltpu.roll(centre, width - 1, 1)
        diagonal = (6.0 * kinetic_scale + vloc_ref[z, pl.ds(y, 1), :]) - energy
        return diagonal * centre - kinetic_scale * beside + dot3(coefficients, u(z, y), NN)

    inner = reduce_end(red_slots.at[0], copies, 1)
    coefficients0 = split(inner * coupling)
    for copy in halos:
        copy.wait_recv()

    def first_apply(z, carry):
        inner, norm = carry
        for y in range(rows):
            first = shifted(pad0, coefficients0, z, y)
            pad1[z + 1, y + 1] = first
            inner = inner + dot3(split(first), u(z, y), NT)
            norm = norm + first * first
        return inner, norm

    carry = first_apply(planes - 1, first_apply(0, (zero_inner, zero_field)))
    halos = halo_start(pad1, 1, (0, 1))
    inner, norm = lax.fori_loop(1, planes - 1, first_apply, carry)
    halos += halo_start(pad1, 1, (2, 3))
    copies = reduce_start(red_slots.at[1], 2, inner)
    first0_part = jnp.sum(norm, axis=1, keepdims=True)
    inner = reduce_end(red_slots.at[1], copies, 2)
    coefficients1 = split(inner * coupling)
    for copy in halos[2:]:
        copy.wait_recv()

    def second_apply(z, correlation):
        for y in range(rows):
            target = shifted(pad1, coefficients1, z, y) + freq_square * pad0[z + 1, y + 1]
            work[z, y] = target
            correlation = correlation + dot3(split(target), phi(z, y), NT)
        return correlation

    correlation = lax.fori_loop(
        1, planes - 1, second_apply, jnp.zeros((count, total_orbs), f32)
    )
    for copy in halos[:2]:
        copy.wait_recv()
    correlation = second_apply(planes - 1, second_apply(0, correlation))
    outer = plane_start(work.at[0], work.at[planes - 1], tz.at[0], tz.at[1], orbs + 1)
    lane = lax.broadcasted_iota(jnp.int32, (count, atoms), 1)

    def scalars(parts):
        out = jnp.zeros((count, atoms), f32)
        for k, part in enumerate(parts):
            out = jnp.where(lane == k, part, out)
        return out

    tail = scalars((norm0_part, first0_part))[:, : red_slots.shape[3] - total_orbs]
    copies = reduce_start(red_slots.at[2], 3, jnp.concatenate([correlation, tail], axis=1))
    total = reduce_end(red_slots.at[2], copies, 3)
    norm0 = total[:, total_orbs : total_orbs + 1]
    first0 = total[:, total_orbs + 1 : total_orbs + 2]
    step0 = norm0 / (first0 + freq_square * norm0)
    g = solve(total[:, :total_orbs] * (1.0 / cells))

    def second_residual(z, carry):
        inner, norm, cross = carry
        for y in range(rows):
            before = pad0[z + 1, y + 1]
            image = work[z, y] - dot3(g, phi(z, y), NN)
            r = before - step0 * image
            pad2[z + 1, y + 1] = r
            inner = inner + dot3(split(r), u(z, y), NT)
            norm = norm + r * r
            cross = cross + r * before
        return inner, norm, cross

    inner, norm, cross = lax.fori_loop(
        0, planes, second_residual, (zero_inner, zero_field, zero_field)
    )
    halos = halo_start(pad2, 2, (2, 3))
    copies = reduce_start(red_slots.at[3], 4, inner)
    norm1_part = jnp.sum(norm, axis=1, keepdims=True)
    cross_part = jnp.sum(cross, axis=1, keepdims=True)
    for copy in outer:
        copy.wait_recv()
    for side, at in ((0, 0), (1, planes + 1)):
        for y in range(rows):
            image = tz[side, y] - dot3(g, phi_beside(side, y), NN)
            pad2[at, y + 1] = pad0[at, y + 1] - step0 * image
    inner = reduce_end(red_slots.at[3], copies, 4)
    coefficients2 = split(inner * coupling)
    for copy in halos:
        copy.wait_recv()

    def third_apply(z, carry):
        square, cross = carry
        for y in range(rows):
            first = shifted(pad2, coefficients2, z, y)
            resp_ref[z, y] = first
            square = square + first * first
            cross = cross + first * pad1[z + 1, y + 1]
        return square, cross

    square, cross = lax.fori_loop(0, planes, third_apply, (zero_field, zero_field))
    square_part = jnp.sum(square, axis=1, keepdims=True)
    mixed_part = jnp.sum(cross, axis=1, keepdims=True)
    copies = reduce_start(
        red_slots.at[4], 5, scalars((norm1_part, cross_part, square_part, mixed_part))
    )
    total = reduce_end(red_slots.at[4], copies, 5)
    norm1, cross, square, mixed = (total[:, k : k + 1] for k in range(4))
    ratio = norm1 / norm0
    curvature = (
        square + 2.0 * ratio * mixed + ratio * ratio * first0
        + freq_square * (norm1 + 2.0 * ratio * cross + ratio * ratio * norm0)
    )
    step1 = norm1 / curvature
    scale0 = step0 + step1 * ratio

    def finish(z, carry):
        for y in range(rows):
            response = scale0 * pad1[z + 1, y + 1] + step1 * resp_ref[z, y]
            resp_ref[z, y] = response
            dens_slots[0, z, pl.ds(y, 1), :] = jnp.sum(
                orb_ref[z, y] * response, axis=0, keepdims=True
            )
        return carry

    lax.fori_loop(0, planes, finish, 0)
    last = [
        start(dens_slots.at[0], dens_slots.at[k], dens_send.at[k - 1], dens_recv.at[k - 1],
              {"orb": lax.rem(orb + k, orbs)})
        for k in range(1, orbs)
    ]
    for copy in last:
        copy.wait_recv()
    density = dens_slots[0]
    for k in range(1, orbs):
        density = density + dens_slots[k]
    dens_ref[...] = density * (4.0 / total_orbs)
    for copy in sent:
        copy.wait_send()


def solution(mesh):
    slabs, pens, orbs = mesh.shape["slab"], mesh.shape["pen"], mesh.shape["orb"]

    def on_device(
        orbitals, energies, frequency, local_potential, perturbation, projectors, profiles,
        couplings, atom_planes,
    ):
        count, planes, rows, width = orbitals.shape
        atoms = projectors.shape[0]
        total_orbs, group = count * orbs, slabs * pens
        table = jnp.concatenate([profiles, atom_planes[:, None].astype(f32)], axis=1)
        vmem = pl.BlockSpec(memory_space=pltpu.VMEM)
        smem = pl.BlockSpec(memory_space=pltpu.SMEM)
        dma = pltpu.SemaphoreType.DMA
        response, density = pl.pallas_call(
            functools.partial(kernel, slabs, pens, orbs),
            out_shape=(
                jax.ShapeDtypeStruct((planes, rows, count, width), f32),
                jax.ShapeDtypeStruct((planes, rows, width), f32),
            ),
            in_specs=[vmem, vmem, smem, vmem, vmem, vmem, vmem, vmem],
            out_specs=(vmem, vmem),
            scratch_shapes=[
                pltpu.VMEM((orbs - 1, planes, rows, count, width), f32),
                pltpu.VMEM((2, orbs, rows, count, width), f32),
                pltpu.VMEM((2, rows, total_orbs, width), bf16),
                pltpu.VMEM((2, rows, total_orbs, width), bf16),
                pltpu.VMEM((2, rows, width), f32),
                pltpu.VMEM((2, rows, count, width), f32),
                pltpu.VMEM((planes, rows, total_orbs, width), bf16),
                pltpu.VMEM((planes, rows, total_orbs, width), bf16),
                pltpu.VMEM((planes, rows, atoms, width), bf16),
                pltpu.VMEM((planes, rows, atoms, width), bf16),
                pltpu.VMEM((planes + 2, rows + 2, count, width), f32),
                pltpu.VMEM((planes + 2, rows + 2, count, width), f32),
                pltpu.VMEM((planes + 2, rows + 2, count, width), f32),
                pltpu.VMEM((planes, rows, count, width), f32),
                pltpu.VMEM((orbs, planes, rows, width), f32),
                pltpu.VMEM((group, (total_orbs + count) // 2, 2 * total_orbs), f32),
                pltpu.VMEM((5, group, count, atoms), f32),
                dma((orbs - 1, 3)), dma((orbs - 1, 3)),
                dma((orbs + 2, 2)), dma((orbs + 2, 2)),
                dma((3, 4)), dma((3, 4)),
                dma((6, group - 1)), dma((6, group - 1)),
                dma((orbs - 1,)), dma((orbs - 1,)),
            ],
            compiler_params=pltpu.CompilerParams(collective_id=0, has_side_effects=True),
        )(
            jnp.transpose(orbitals, (1, 2, 0, 3)),
            energies[:, None],
            frequency,
            local_potential,
            perturbation,
            jnp.transpose(projectors, (1, 0, 2)),
            table,
            couplings[None, :],
        )
        return jnp.transpose(response, (2, 0, 1, 3)), density

    in_specs = (
        P(("parts", "orb"), "slab", "pen", None), P(("parts", "orb")), P("parts"),
        P("slab", "pen", None), P("slab", "pen", None), P(None, "pen", None), P(), P(), P(),
    )
    out_specs = (P(("parts", "orb"), "slab", "pen", None), P(("parts", "slab"), "pen", None))
    return jax.shard_map(
        on_device, mesh=mesh, in_specs=in_specs, out_specs=out_specs, check_vma=False
    )
```

```python
import functools

import jax
import jax.numpy as jnp
from jax import lax
from jax.experimental import pallas as pl
from jax.experimental.pallas import tpu as pltpu
from jax.sharding import PartitionSpec as P

kinetic_scale = 0.125
MESH = pl.DeviceIdType.MESH
f32, bf16 = jnp.float32, jnp.bfloat16
NT = (((1,), (1,)), ((), ()))
NN = (((1,), (0,)), ((), ()))


def split(x):
    hi = x.astype(bf16)
    return hi, (x - hi.astype(f32)).astype(bf16)


def dot3(a, b, dims):
    rows = a[0].shape[0]
    both = lax.dot_general(jnp.concatenate(a, axis=0), b[0], dims, preferred_element_type=f32)
    rest = lax.dot_general(a[0], b[1], dims, preferred_element_type=f32)
    return both[:rows] + both[rows:] + rest


def inverse(a):
    size = a.shape[0]
    row_id = lax.broadcasted_iota(jnp.int32, (size, size), 0)
    col_id = lax.broadcasted_iota(jnp.int32, (size, size), 1)
    lane = lax.broadcasted_iota(jnp.int32, (1, size), 1)
    diagonal = jnp.where(row_id == col_id, a, 0.0)
    scale = (1.0 / jnp.sqrt(jnp.sum(diagonal, axis=1, keepdims=True))) * (
        1.0 / jnp.sqrt(jnp.sum(diagonal, axis=0, keepdims=True))
    )
    a = a * scale
    for k in range(0, size, 2):
        p, q = a[k : k + 1, k : k + 1], a[k : k + 1, k + 1 : k + 2]
        r, t = a[k + 1 : k + 2, k : k + 1], a[k + 1 : k + 2, k + 1 : k + 2]
        top, low = a[k : k + 1, :], a[k + 1 : k + 2, :]
        first, second = a[:, k : k + 1], a[:, k + 1 : k + 2]
        inv = 1.0 / (p * t - q * r)
        new_top = jnp.where(lane == k, t, jnp.where(lane == k + 1, -q, t * top - q * low)) * inv
        new_low = jnp.where(lane == k, -r, jnp.where(lane == k + 1, p, p * low - r * top)) * inv
        rest = jnp.where((col_id == k) | (col_id == k + 1), 0.0, a)
        rest = rest - first * new_top - second * new_low
        a = jnp.where(row_id == k, new_top, jnp.where(row_id == k + 1, new_low, rest))
    return a * scale


def kernel(
    slabs, pens, orbs, orb_ref, en_ref, freq_ref, vloc_ref, dv_ref, beta_ref, prof_ref, atom_ref, coup_ref,
    resp_ref, dens_ref,
    others, phz, phz_hi, phz_lo, dvz, tz, phi_hi, phi_lo, u_hi, u_lo, pad0, pad1, pad2, work, dens_slots,
    gram_slots, red_slots,
    gather_send, gather_recv, plane_send, plane_recv, halo_send, halo_recv, red_send, red_recv, dens_send, dens_recv,
):
    planes, rows, count, width = orb_ref.shape
    atoms = beta_ref.shape[0]
    span = prof_ref.shape[0]
    total_orbs = count * orbs
    depth = planes * slabs
    cells = float(depth * rows * pens * width)
    slab, pen, orb = lax.axis_index("slab"), lax.axis_index("pen"), lax.axis_index("orb")
    group = slabs * pens
    me = slab * pens + pen

    def peer(k):
        target = lax.rem(me + k, group)
        return {"slab": target // pens, "pen": lax.rem(target, pens)}

    barrier = pltpu.get_barrier_semaphore()
    for k in range(1, group):
        pl.semaphore_signal(barrier, inc=1, device_id=peer(k), device_id_type=MESH)
    for k in range(1, orbs):
        pl.semaphore_signal(
            barrier, inc=1, device_id={"orb": lax.rem(orb + k, orbs)}, device_id_type=MESH
        )
    pl.semaphore_wait(barrier, group - 1 + orbs - 1)

    sent = []

    def start(src, dst, send, recv, device):
        copy = pltpu.make_async_remote_copy(
            src_ref=src, dst_ref=dst, send_sem=send, recv_sem=recv,
            device_id=device, device_id_type=MESH,
        )
        copy.start()
        sent.append(copy)
        return copy

    pieces = [pl.ds(0, 1), pl.ds(planes - 1, 1)]
    if planes > 2:
        pieces.append(pl.ds(1, planes - 2))
    gathers = [
        [
            start(orb_ref.at[piece], others.at[k - 1, piece], gather_send.at[k - 1, n],
                  gather_recv.at[k - 1, n], {"orb": lax.rem(orb + k, orbs)})
            for k in range(1, orbs)
        ]
        for n, piece in enumerate(pieces)
    ]

    up, down = lax.rem(slab + 1, slabs), lax.rem(slab + slabs - 1, slabs)

    def plane_start(low, high, below, above, index):
        return [
            start(low, above, plane_send.at[index, 0], plane_recv.at[index, 0], {"slab": down}),
            start(high, below, plane_send.at[index, 1], plane_recv.at[index, 1], {"slab": up}),
        ]

    beside = plane_start(
        dv_ref.at[0], dv_ref.at[planes - 1], dvz.at[0], dvz.at[1], orbs
    ) + plane_start(
        orb_ref.at[0], orb_ref.at[planes - 1], phz.at[0, 0], phz.at[1, 0], 0
    )

    def halo_start(pad, index, wanted):
        right, left = lax.rem(pen + 1, pens), lax.rem(pen + pens - 1, pens)
        inner_p, inner_r = pl.ds(1, planes), pl.ds(1, rows)
        sides = (
            (pad.at[planes, inner_r], pad.at[0, inner_r], {"slab": up}),
            (pad.at[1, inner_r], pad.at[planes + 1, inner_r], {"slab": down}),
            (pad.at[inner_p, rows], pad.at[inner_p, 0], {"pen": right}),
            (pad.at[inner_p, 1], pad.at[inner_p, rows + 1], {"pen": left}),
        )
        return [
            start(src, dst, halo_send.at[index, side], halo_recv.at[index, side], device)
            for side, (src, dst, device) in enumerate(sides)
            if side in wanted
        ]

    def reduce_start(slots, index, values):
        slots[me] = values
        return [
            start(slots.at[me], slots.at[me], red_send.at[index, k - 1], red_recv.at[index, k - 1],
                  peer(k))
            for k in range(1, group)
        ]

    def reduce_end(slots, copies, index):
        for k in range(1, group):
            source = lax.rem(me + group - k, group)
            pltpu.make_async_remote_copy(
                src_ref=slots.at[source], dst_ref=slots.at[source],
                send_sem=red_send.at[index, k - 1], recv_sem=red_recv.at[index, k - 1],
                device_id=peer(k), device_id_type=MESH,
            ).wait_recv()
        total = slots[0]
        for k in range(1, group):
            total = total + slots[k]
        return total

    def as_column(row):
        size = row.shape[1]
        row_id = lax.broadcasted_iota(jnp.int32, (size, size), 0)
        col_id = lax.broadcasted_iota(jnp.int32, (size, size), 1)
        return jnp.sum(jnp.where(row_id == col_id, row, 0.0), axis=1, keepdims=True)

    atom = atom_ref[...]
    for z in range(planes):
        plane = slab * planes + z
        weight = jnp.zeros((1, atoms), f32)
        for d in range(span):
            covered = atom + d
            covered = jnp.where(covered >= depth, covered - depth, covered)
            weight = weight + jnp.where(covered == plane, prof_ref[d : d + 1, :], 0.0)
        weight = as_column(weight)
        for y in range(rows):
            hi, lo = split(beta_ref[:, y, :] * weight)
            u_hi[z, y] = hi
            u_lo[z, y] = lo

    for piece in gathers[:2]:
        for copy in piece:
            copy.wait_recv()
    for k in range(1, orbs):
        beside += plane_start(
            others.at[k - 1, 0], others.at[k - 1, planes - 1], phz.at[0, k], phz.at[1, k], k
        )
    for piece in gathers[2:]:
        for copy in piece:
            copy.wait_recv()

    def put_phi(z, carry):
        for y in range(rows):
            for k in range(orbs):
                hi, lo = split(orb_ref[z, y] if k == 0 else others[k - 1, z, y])
                phi_hi[z, y, k * count : (k + 1) * count] = hi
                phi_lo[z, y, k * count : (k + 1) * count] = lo
        return carry

    lax.fori_loop(0, planes, put_phi, 0)

    def phi(z, y):
        return phi_hi[z, y], phi_lo[z, y]

    def u(z, y):
        return u_hi[z, y], u_lo[z, y]

    def gram_part(z, acc):
        for y in range(rows):
            source = dv_ref[z, pl.ds(y, 1), :] * orb_ref[z, y]
            s_hi, s_lo = split(source)
            left = (
                jnp.concatenate([phi_hi[z, y], s_hi], axis=0),
                jnp.concatenate([phi_lo[z, y], s_lo], axis=0),
            )
            acc = acc + dot3(left, phi(z, y), NT)
        return acc

    part = lax.fori_loop(0, planes, gram_part, jnp.zeros((total_orbs + count, total_orbs), f32))
    half = (total_orbs + count) // 2
    packed = jnp.concatenate([part[:half], part[half:]], axis=1)
    copies = reduce_start(gram_slots, 0, packed)
    packed = reduce_end(gram_slots, copies, 0) * (1.0 / cells)
    full = jnp.concatenate([packed[:, :total_orbs], packed[:, total_orbs:]], axis=0)
    gram_inverse = split(inverse(full[:total_orbs]))

    def solve(correlation):
        return split(dot3(split(correlation), gram_inverse, NN))

    zero_field = jnp.zeros((count, width), f32)
    zero_inner = jnp.zeros((count, atoms), f32)
    energy = as_column(en_ref[...])
    coupling = coup_ref[...]
    freq_square = freq_ref[0] * freq_ref[0]

    g = solve(full[total_orbs:])

    def first_residual(z, carry):
        inner, norm = carry
        for y in range(rows):
            source = dv_ref[z, pl.ds(y, 1), :] * orb_ref[z, y]
            r = dot3(g, phi(z, y), NN) - source
            pad0[z + 1, y + 1] = r
            inner = inner + dot3(split(r), u(z, y), NT)
            norm = norm + r * r
        return inner, norm

    inner, norm = lax.fori_loop(0, planes, first_residual, (zero_inner, zero_field))
    halos = halo_start(pad0, 0, (2, 3))
    copies = reduce_start(red_slots.at[0], 1, inner)
    norm0_part = jnp.sum(norm, axis=1, keepdims=True)
    for copy in beside:
        copy.wait_recv()

    def phi_beside(side, y):
        return phz_hi[side, y], phz_lo[side, y]

    for side, at in ((0, 0), (1, planes + 1)):
        for y in range(rows):
            for k in range(orbs):
                hi, lo = split(phz[side, k, y])
                phz_hi[side, y, k * count : (k + 1) * count] = hi
                phz_lo[side, y, k * count : (k + 1) * count] = lo
            source = dvz[side, y : y + 1, :] * phz[side, 0, y]
            pad0[at, y + 1] = dot3(g, phi_beside(side, y), NN) - source

    def shifted(pad, coefficients, z, y):
        centre = pad[z + 1, y + 1]
        beside = pad[z, y + 1] + pad[z + 2, y + 1] + pad[z + 1, y] + pad[z + 1, y + 2]
        beside = beside + pltpu.roll(centre, 1, 1) + pltpu.roll(centre, width - 1, 1)
        diagonal = (6.0 * kinetic_scale + vloc_ref[z, pl.ds(y, 1), :]) - energy
        return diagonal * centre - kinetic_scale * beside + dot3(coefficients, u(z, y), NN)

    inner = reduce_end(red_slots.at[0], copies, 1)
    coefficients0 = split(inner * coupling)
    for copy in halos:
        copy.wait_recv()

    def first_apply(z, carry):
        inner, norm = carry
        for y in range(rows):
            first = shifted(pad0, coefficients0, z, y)
            pad1[z + 1, y + 1] = first
            inner = inner + dot3(split(first), u(z, y), NT)
            norm = norm + first * first
        return inner, norm

    carry = first_apply(planes - 1, first_apply(0, (zero_inner, zero_field)))
    halos = halo_start(pad1, 1, (0, 1))
    inner, norm = lax.fori_loop(1, planes - 1, first_apply, carry)
    halos += halo_start(pad1, 1, (2, 3))
    copies = reduce_start(red_slots.at[1], 2, inner)
    first0_part = jnp.sum(norm, axis=1, keepdims=True)
    inner = reduce_end(red_slots.at[1], copies, 2)
    coefficients1 = split(inner * coupling)
    for copy in halos[2:]:
        copy.wait_recv()

    def second_apply(z, correlation):
        for y in range(rows):
            target = shifted(pad1, coefficients1, z, y) + freq_square * pad0[z + 1, y + 1]
            work[z, y] = target
            correlation = correlation + dot3(split(target), phi(z, y), NT)
        return correlation

    correlation = lax.fori_loop(
        1, planes - 1, second_apply, jnp.zeros((count, total_orbs), f32)
    )
    for copy in halos[:2]:
        copy.wait_recv()
    correlation = second_apply(planes - 1, second_apply(0, correlation))
    outer = plane_start(work.at[0], work.at[planes - 1], tz.at[0], tz.at[1], orbs + 1)
    lane = lax.broadcasted_iota(jnp.int32, (count, atoms), 1)

    def scalars(parts):
        out = jnp.zeros((count, atoms), f32)
        for k, part in enumerate(parts):
            out = jnp.where(lane == k, part, out)
        return out

    tail = scalars((norm0_part, first0_part))[:, : red_slots.shape[3] - total_orbs]
    copies = reduce_start(red_slots.at[2], 3, jnp.concatenate([correlation, tail], axis=1))
    total = reduce_end(red_slots.at[2], copies, 3)
    norm0 = total[:, total_orbs : total_orbs + 1]
    first0 = total[:, total_orbs + 1 : total_orbs + 2]
    step0 = norm0 / (first0 + freq_square * norm0)
    g = solve(total[:, :total_orbs] * (1.0 / cells))

    def second_residual(z, carry):
        inner, norm, cross = carry
        for y in range(rows):
            before = pad0[z + 1, y + 1]
            image = work[z, y] - dot3(g, phi(z, y), NN)
            r = before - step0 * image
            pad2[z + 1, y + 1] = r
            inner = inner + dot3(split(r), u(z, y), NT)
            norm = norm + r * r
            cross = cross + r * before
        return inner, norm, cross

    inner, norm, cross = lax.fori_loop(
        0, planes, second_residual, (zero_inner, zero_field, zero_field)
    )
    halos = halo_start(pad2, 2, (2, 3))
    copies = reduce_start(red_slots.at[3], 4, inner)
    norm1_part = jnp.sum(norm, axis=1, keepdims=True)
    cross_part = jnp.sum(cross, axis=1, keepdims=True)
    for copy in outer:
        copy.wait_recv()
    for side, at in ((0, 0), (1, planes + 1)):
        for y in range(rows):
            image = tz[side, y] - dot3(g, phi_beside(side, y), NN)
            pad2[at, y + 1] = pad0[at, y + 1] - step0 * image
    inner = reduce_end(red_slots.at[3], copies, 4)
    coefficients2 = split(inner * coupling)
    for copy in halos:
        copy.wait_recv()

    def third_apply(z, carry):
        square, cross = carry
        for y in range(rows):
            first = shifted(pad2, coefficients2, z, y)
            resp_ref[z, y] = first
            square = square + first * first
            cross = cross + first * pad1[z + 1, y + 1]
        return square, cross

    square, cross = lax.fori_loop(0, planes, third_apply, (zero_field, zero_field))
    square_part = jnp.sum(square, axis=1, keepdims=True)
    mixed_part = jnp.sum(cross, axis=1, keepdims=True)
    copies = reduce_start(
        red_slots.at[4], 5, scalars((norm1_part, cross_part, square_part, mixed_part))
    )
    total = reduce_end(red_slots.at[4], copies, 5)
    norm1, cross, square, mixed = (total[:, k : k + 1] for k in range(4))
    ratio = norm1 / norm0
    curvature = (
        square + 2.0 * ratio * mixed + ratio * ratio * first0
        + freq_square * (norm1 + 2.0 * ratio * cross + ratio * ratio * norm0)
    )
    step1 = norm1 / curvature
    scale0 = step0 + step1 * ratio

    def finish(z, carry):
        for y in range(rows):
            response = scale0 * pad1[z + 1, y + 1] + step1 * resp_ref[z, y]
            resp_ref[z, y] = response
            dens_slots[0, z, pl.ds(y, 1), :] = jnp.sum(
                orb_ref[z, y] * response, axis=0, keepdims=True
            )
        return carry

    lax.fori_loop(0, planes, finish, 0)
    last = [
        start(dens_slots.at[0], dens_slots.at[k], dens_send.at[k - 1], dens_recv.at[k - 1],
              {"orb": lax.rem(orb + k, orbs)})
        for k in range(1, orbs)
    ]
    for copy in last:
        copy.wait_recv()
    density = dens_slots[0]
    for k in range(1, orbs):
        density = density + dens_slots[k]
    dens_ref[...] = density * (4.0 / total_orbs)
    for copy in sent:
        copy.wait_send()


def solution(mesh):
    slabs, pens, orbs = mesh.shape["slab"], mesh.shape["pen"], mesh.shape["orb"]

    def on_device(
        orbitals, energies, frequency, local_potential, perturbation, projectors, profiles,
        couplings, atom_planes,
    ):
        count, planes, rows, width = orbitals.shape
        atoms = projectors.shape[0]
        total_orbs, group = count * orbs, slabs * pens
        vmem = pl.BlockSpec(memory_space=pltpu.VMEM)
        smem = pl.BlockSpec(memory_space=pltpu.SMEM)
        dma = pltpu.SemaphoreType.DMA
        response, density = pl.pallas_call(
            functools.partial(kernel, slabs, pens, orbs),
            out_shape=(
                jax.ShapeDtypeStruct((planes, rows, count, width), f32),
                jax.ShapeDtypeStruct((planes, rows, width), f32),
            ),
            in_specs=[vmem, vmem, smem, vmem, vmem, vmem, vmem, vmem, vmem],
            out_specs=(vmem, vmem),
            scratch_shapes=[
                pltpu.VMEM((orbs - 1, planes, rows, count, width), f32),
                pltpu.VMEM((2, orbs, rows, count, width), f32),
                pltpu.VMEM((2, rows, total_orbs, width), bf16),
                pltpu.VMEM((2, rows, total_orbs, width), bf16),
                pltpu.VMEM((2, rows, width), f32),
                pltpu.VMEM((2, rows, count, width), f32),
                pltpu.VMEM((planes, rows, total_orbs, width), bf16),
                pltpu.VMEM((planes, rows, total_orbs, width), bf16),
                pltpu.VMEM((planes, rows, atoms, width), bf16),
                pltpu.VMEM((planes, rows, atoms, width), bf16),
                pltpu.VMEM((planes + 2, rows + 2, count, width), f32),
                pltpu.VMEM((planes + 2, rows + 2, count, width), f32),
                pltpu.VMEM((planes + 2, rows + 2, count, width), f32),
                pltpu.VMEM((planes, rows, count, width), f32),
                pltpu.VMEM((orbs, planes, rows, width), f32),
                pltpu.VMEM((group, (total_orbs + count) // 2, 2 * total_orbs), f32),
                pltpu.VMEM((5, group, count, atoms), f32),
                dma((orbs - 1, 3)), dma((orbs - 1, 3)),
                dma((orbs + 2, 2)), dma((orbs + 2, 2)),
                dma((3, 4)), dma((3, 4)),
                dma((6, group - 1)), dma((6, group - 1)),
                dma((orbs - 1,)), dma((orbs - 1,)),
            ],
            compiler_params=pltpu.CompilerParams(collective_id=0, has_side_effects=True),
        )(
            jnp.transpose(orbitals, (1, 2, 0, 3)),
            energies[None, :],
            frequency,
            local_potential,
            perturbation,
            projectors,
            profiles.T,
            atom_planes[None, :],
            couplings[None, :],
        )
        return jnp.transpose(response, (2, 0, 1, 3)), density

    in_specs = (
        P(("parts", "orb"), "slab", "pen", None), P(("parts", "orb")), P("parts"),
        P("slab", "pen", None), P("slab", "pen", None), P(None, "pen", None), P(), P(), P(),
    )
    out_specs = (P(("parts", "orb"), "slab", "pen", None), P(("parts", "slab"), "pen", None))
    return jax.shard_map(
        on_device, mesh=mesh, in_specs=in_specs, out_specs=out_specs, check_vma=False
    )
```

```python
import functools

import jax
import jax.numpy as jnp
from jax import lax
from jax.experimental import pallas as pl
from jax.experimental.pallas import tpu as pltpu
from jax.sharding import PartitionSpec as P

kinetic_scale = 0.125
MESH = pl.DeviceIdType.MESH
f32, bf16 = jnp.float32, jnp.bfloat16
NT = (((1,), (1,)), ((), ()))
NN = (((1,), (0,)), ((), ()))


def split(x):
    hi = x.astype(bf16)
    return hi, (x - hi.astype(f32)).astype(bf16)


def dot3(a, b, dims):
    rows = a[0].shape[0]
    both = lax.dot_general(jnp.concatenate(a, axis=0), b[0], dims, preferred_element_type=f32)
    rest = lax.dot_general(a[0], b[1], dims, preferred_element_type=f32)
    return both[:rows] + both[rows:] + rest


def inverse(a):
    size = a.shape[0]
    row_id = lax.broadcasted_iota(jnp.int32, (size, size), 0)
    col_id = lax.broadcasted_iota(jnp.int32, (size, size), 1)
    lane = lax.broadcasted_iota(jnp.int32, (1, size), 1)
    diagonal = jnp.where(row_id == col_id, a, 0.0)
    scale = (1.0 / jnp.sqrt(jnp.sum(diagonal, axis=1, keepdims=True))) * (
        1.0 / jnp.sqrt(jnp.sum(diagonal, axis=0, keepdims=True))
    )
    a = a * scale
    for k in range(0, size, 2):
        p, q = a[k : k + 1, k : k + 1], a[k : k + 1, k + 1 : k + 2]
        r, t = a[k + 1 : k + 2, k : k + 1], a[k + 1 : k + 2, k + 1 : k + 2]
        top, low = a[k : k + 1, :], a[k + 1 : k + 2, :]
        first, second = a[:, k : k + 1], a[:, k + 1 : k + 2]
        inv = 1.0 / (p * t - q * r)
        new_top = jnp.where(lane == k, t, jnp.where(lane == k + 1, -q, t * top - q * low)) * inv
        new_low = jnp.where(lane == k, -r, jnp.where(lane == k + 1, p, p * low - r * top)) * inv
        rest = jnp.where((col_id == k) | (col_id == k + 1), 0.0, a)
        rest = rest - first * new_top - second * new_low
        a = jnp.where(row_id == k, new_top, jnp.where(row_id == k + 1, new_low, rest))
    return a * scale


def loop(low, high, body, carry):
    for z in range(low, high):
        carry = body(z, carry)
    return carry


def kernel(
    slabs, pens, orbs, orb_ref, en_ref, freq_ref, vloc_ref, dv_ref, beta_ref, prof_ref, atom_ref, coup_ref,
    resp_ref, dens_ref,
    others, phz, phz_hi, phz_lo, dvz, tz, phi_hi, phi_lo, u_hi, u_lo, pad0, pad1, pad2, work, dens_slots,
    gram_slots, red_slots,
    gather_send, gather_recv, plane_send, plane_recv, halo_send, halo_recv, red_send, red_recv, dens_send, dens_recv,
):
    planes, rows, count, width = orb_ref.shape
    atoms = beta_ref.shape[0]
    span = prof_ref.shape[0]
    total_orbs = count * orbs
    depth = planes * slabs
    cells = float(depth * rows * pens * width)
    slab, pen, orb = lax.axis_index("slab"), lax.axis_index("pen"), lax.axis_index("orb")
    group = slabs * pens
    me = slab * pens + pen

    def peer(k):
        target = lax.rem(me + k, group)
        return {"slab": target // pens, "pen": lax.rem(target, pens)}

    barrier = pltpu.get_barrier_semaphore()
    for k in range(1, group):
        pl.semaphore_signal(barrier, inc=1, device_id=peer(k), device_id_type=MESH)
    for k in range(1, orbs):
        pl.semaphore_signal(
            barrier, inc=1, device_id={"orb": lax.rem(orb + k, orbs)}, device_id_type=MESH
        )
    pl.semaphore_wait(barrier, group - 1 + orbs - 1)

    sent = []

    def start(src, dst, send, recv, device):
        copy = pltpu.make_async_remote_copy(
            src_ref=src, dst_ref=dst, send_sem=send, recv_sem=recv,
            device_id=device, device_id_type=MESH,
        )
        copy.start()
        sent.append(copy)
        return copy

    pieces = [pl.ds(0, 1), pl.ds(planes - 1, 1)]
    if planes > 2:
        pieces.append(pl.ds(1, planes - 2))
    gathers = [
        [
            start(orb_ref.at[piece], others.at[k - 1, piece], gather_send.at[k - 1, n],
                  gather_recv.at[k - 1, n], {"orb": lax.rem(orb + k, orbs)})
            for k in range(1, orbs)
        ]
        for n, piece in enumerate(pieces)
    ]

    up, down = lax.rem(slab + 1, slabs), lax.rem(slab + slabs - 1, slabs)

    def plane_start(low, high, below, above, index):
        return [
            start(low, above, plane_send.at[index, 0], plane_recv.at[index, 0], {"slab": down}),
            start(high, below, plane_send.at[index, 1], plane_recv.at[index, 1], {"slab": up}),
        ]

    beside = plane_start(
        dv_ref.at[0], dv_ref.at[planes - 1], dvz.at[0], dvz.at[1], orbs
    ) + plane_start(
        orb_ref.at[0], orb_ref.at[planes - 1], phz.at[0, 0], phz.at[1, 0], 0
    )

    def halo_start(pad, index, wanted):
        right, left = lax.rem(pen + 1, pens), lax.rem(pen + pens - 1, pens)
        inner_p, inner_r = pl.ds(1, planes), pl.ds(1, rows)
        sides = (
            (pad.at[planes, inner_r], pad.at[0, inner_r], {"slab": up}),
            (pad.at[1, inner_r], pad.at[planes + 1, inner_r], {"slab": down}),
            (pad.at[inner_p, rows], pad.at[inner_p, 0], {"pen": right}),
            (pad.at[inner_p, 1], pad.at[inner_p, rows + 1], {"pen": left}),
        )
        return [
            start(src, dst, halo_send.at[index, side], halo_recv.at[index, side], device)
            for side, (src, dst, device) in enumerate(sides)
            if side in wanted
        ]

    def reduce_start(slots, index, values):
        slots[me] = values
        return [
            start(slots.at[me], slots.at[me], red_send.at[index, k - 1], red_recv.at[index, k - 1],
                  peer(k))
            for k in range(1, group)
        ]

    def reduce_end(slots, copies, index):
        for k in range(1, group):
            source = lax.rem(me + group - k, group)
            pltpu.make_async_remote_copy(
                src_ref=slots.at[source], dst_ref=slots.at[source],
                send_sem=red_send.at[index, k - 1], recv_sem=red_recv.at[index, k - 1],
                device_id=peer(k), device_id_type=MESH,
            ).wait_recv()
        total = slots[0]
        for k in range(1, group):
            total = total + slots[k]
        return total

    def as_column(row):
        size = row.shape[1]
        row_id = lax.broadcasted_iota(jnp.int32, (size, size), 0)
        col_id = lax.broadcasted_iota(jnp.int32, (size, size), 1)
        return jnp.sum(jnp.where(row_id == col_id, row, 0.0), axis=1, keepdims=True)

    atom = atom_ref[...]
    for z in range(planes):
        plane = slab * planes + z
        weight = jnp.zeros((1, atoms), f32)
        for d in range(span):
            covered = atom + d
            covered = jnp.where(covered >= depth, covered - depth, covered)
            weight = weight + jnp.where(covered == plane, prof_ref[d : d + 1, :], 0.0)
        weight = as_column(weight)
        for y in range(rows):
            hi, lo = split(beta_ref[:, y, :] * weight)
            u_hi[z, y] = hi
            u_lo[z, y] = lo

    for piece in gathers[:2]:
        for copy in piece:
            copy.wait_recv()
    for k in range(1, orbs):
        beside += plane_start(
            others.at[k - 1, 0], others.at[k - 1, planes - 1], phz.at[0, k], phz.at[1, k], k
        )
    for piece in gathers[2:]:
        for copy in piece:
            copy.wait_recv()

    def put_phi(z, carry):
        for y in range(rows):
            for k in range(orbs):
                hi, lo = split(orb_ref[z, y] if k == 0 else others[k - 1, z, y])
                phi_hi[z, y, k * count : (k + 1) * count] = hi
                phi_lo[z, y, k * count : (k + 1) * count] = lo
        return carry

    loop(0, planes, put_phi, 0)

    def phi(z, y):
        return phi_hi[z, y], phi_lo[z, y]

    def u(z, y):
        return u_hi[z, y], u_lo[z, y]

    def gram_part(z, acc):
        for y in range(rows):
            source = dv_ref[z, pl.ds(y, 1), :] * orb_ref[z, y]
            s_hi, s_lo = split(source)
            left = (
                jnp.concatenate([phi_hi[z, y], s_hi], axis=0),
                jnp.concatenate([phi_lo[z, y], s_lo], axis=0),
            )
            acc = acc + dot3(left, phi(z, y), NT)
        return acc

    part = loop(0, planes, gram_part, jnp.zeros((total_orbs + count, total_orbs), f32))
    half = (total_orbs + count) // 2
    packed = jnp.concatenate([part[:half], part[half:]], axis=1)
    copies = reduce_start(gram_slots, 0, packed)
    packed = reduce_end(gram_slots, copies, 0) * (1.0 / cells)
    full = jnp.concatenate([packed[:, :total_orbs], packed[:, total_orbs:]], axis=0)
    gram_inverse = split(inverse(full[:total_orbs]))

    def solve(correlation):
        return split(dot3(split(correlation), gram_inverse, NN))

    zero_field = jnp.zeros((count, width), f32)
    zero_inner = jnp.zeros((count, atoms), f32)
    energy = as_column(en_ref[...])
    coupling = coup_ref[...]
    freq_square = freq_ref[0] * freq_ref[0]

    g = solve(full[total_orbs:])

    def first_residual(z, carry):
        inner, norm = carry
        for y in range(rows):
            source = dv_ref[z, pl.ds(y, 1), :] * orb_ref[z, y]
            r = dot3(g, phi(z, y), NN) - source
            pad0[z + 1, y + 1] = r
            inner = inner + dot3(split(r), u(z, y), NT)
            norm = norm + r * r
        return inner, norm

    inner, norm = loop(0, planes, first_residual, (zero_inner, zero_field))
    halos = halo_start(pad0, 0, (2, 3))
    copies = reduce_start(red_slots.at[0], 1, inner)
    norm0_part = jnp.sum(norm, axis=1, keepdims=True)
    for copy in beside:
        copy.wait_recv()

    def phi_beside(side, y):
        return phz_hi[side, y], phz_lo[side, y]

    for side, at in ((0, 0), (1, planes + 1)):
        for y in range(rows):
            for k in range(orbs):
                hi, lo = split(phz[side, k, y])
                phz_hi[side, y, k * count : (k + 1) * count] = hi
                phz_lo[side, y, k * count : (k + 1) * count] = lo
            source = dvz[side, y : y + 1, :] * phz[side, 0, y]
            pad0[at, y + 1] = dot3(g, phi_beside(side, y), NN) - source

    def shifted(pad, coefficients, z, y):
        centre = pad[z + 1, y + 1]
        beside = pad[z, y + 1] + pad[z + 2, y + 1] + pad[z + 1, y] + pad[z + 1, y + 2]
        beside = beside + pltpu.roll(centre, 1, 1) + pltpu.roll(centre, width - 1, 1)
        diagonal = (6.0 * kinetic_scale + vloc_ref[z, pl.ds(y, 1), :]) - energy
        return diagonal * centre - kinetic_scale * beside + dot3(coefficients, u(z, y), NN)

    inner = reduce_end(red_slots.at[0], copies, 1)
    coefficients0 = split(inner * coupling)
    for copy in halos:
        copy.wait_recv()

    def first_apply(z, carry):
        inner, norm = carry
        for y in range(rows):
            first = shifted(pad0, coefficients0, z, y)
            pad1[z + 1, y + 1] = first
            inner = inner + dot3(split(first), u(z, y), NT)
            norm = norm + first * first
        return inner, norm

    carry = first_apply(planes - 1, first_apply(0, (zero_inner, zero_field)))
    halos = halo_start(pad1, 1, (0, 1))
    inner, norm = loop(1, planes - 1, first_apply, carry)
    halos += halo_start(pad1, 1, (2, 3))
    copies = reduce_start(red_slots.at[1], 2, inner)
    first0_part = jnp.sum(norm, axis=1, keepdims=True)
    inner = reduce_end(red_slots.at[1], copies, 2)
    coefficients1 = split(inner * coupling)
    for copy in halos[2:]:
        copy.wait_recv()

    def second_apply(z, correlation):
        for y in range(rows):
            target = shifted(pad1, coefficients1, z, y) + freq_square * pad0[z + 1, y + 1]
            work[z, y] = target
            correlation = correlation + dot3(split(target), phi(z, y), NT)
        return correlation

    correlation = loop(
        1, planes - 1, second_apply, jnp.zeros((count, total_orbs), f32)
    )
    for copy in halos[:2]:
        copy.wait_recv()
    correlation = second_apply(planes - 1, second_apply(0, correlation))
    outer = plane_start(work.at[0], work.at[planes - 1], tz.at[0], tz.at[1], orbs + 1)
    lane = lax.broadcasted_iota(jnp.int32, (count, atoms), 1)

    def scalars(parts):
        out = jnp.zeros((count, atoms), f32)
        for k, part in enumerate(parts):
            out = jnp.where(lane == k, part, out)
        return out

    tail = scalars((norm0_part, first0_part))[:, : red_slots.shape[3] - total_orbs]
    copies = reduce_start(red_slots.at[2], 3, jnp.concatenate([correlation, tail], axis=1))
    total = reduce_end(red_slots.at[2], copies, 3)
    norm0 = total[:, total_orbs : total_orbs + 1]
    first0 = total[:, total_orbs + 1 : total_orbs + 2]
    step0 = norm0 / (first0 + freq_square * norm0)
    g = solve(total[:, :total_orbs] * (1.0 / cells))

    def second_residual(z, carry):
        inner, norm, cross = carry
        for y in range(rows):
            before = pad0[z + 1, y + 1]
            image = work[z, y] - dot3(g, phi(z, y), NN)
            r = before - step0 * image
            pad2[z + 1, y + 1] = r
            inner = inner + dot3(split(r), u(z, y), NT)
            norm = norm + r * r
            cross = cross + r * before
        return inner, norm, cross

    inner, norm, cross = loop(
        0, planes, second_residual, (zero_inner, zero_field, zero_field)
    )
    halos = halo_start(pad2, 2, (2, 3))
    copies = reduce_start(red_slots.at[3], 4, inner)
    norm1_part = jnp.sum(norm, axis=1, keepdims=True)
    cross_part = jnp.sum(cross, axis=1, keepdims=True)
    for copy in outer:
        copy.wait_recv()
    for side, at in ((0, 0), (1, planes + 1)):
        for y in range(rows):
            image = tz[side, y] - dot3(g, phi_beside(side, y), NN)
            pad2[at, y + 1] = pad0[at, y + 1] - step0 * image
    inner = reduce_end(red_slots.at[3], copies, 4)
    coefficients2 = split(inner * coupling)
    for copy in halos:
        copy.wait_recv()

    def third_apply(z, carry):
        square, cross = carry
        for y in range(rows):
            first = shifted(pad2, coefficients2, z, y)
            resp_ref[z, y] = first
            square = square + first * first
            cross = cross + first * pad1[z + 1, y + 1]
        return square, cross

    square, cross = loop(0, planes, third_apply, (zero_field, zero_field))
    square_part = jnp.sum(square, axis=1, keepdims=True)
    mixed_part = jnp.sum(cross, axis=1, keepdims=True)
    copies = reduce_start(
        red_slots.at[4], 5, scalars((norm1_part, cross_part, square_part, mixed_part))
    )
    total = reduce_end(red_slots.at[4], copies, 5)
    norm1, cross, square, mixed = (total[:, k : k + 1] for k in range(4))
    ratio = norm1 / norm0
    curvature = (
        square + 2.0 * ratio * mixed + ratio * ratio * first0
        + freq_square * (norm1 + 2.0 * ratio * cross + ratio * ratio * norm0)
    )
    step1 = norm1 / curvature
    scale0 = step0 + step1 * ratio

    def finish(z, carry):
        for y in range(rows):
            response = scale0 * pad1[z + 1, y + 1] + step1 * resp_ref[z, y]
            resp_ref[z, y] = response
            dens_slots[0, z, pl.ds(y, 1), :] = jnp.sum(
                orb_ref[z, y] * response, axis=0, keepdims=True
            )
        return carry

    loop(0, planes, finish, 0)
    last = [
        start(dens_slots.at[0], dens_slots.at[k], dens_send.at[k - 1], dens_recv.at[k - 1],
              {"orb": lax.rem(orb + k, orbs)})
        for k in range(1, orbs)
    ]
    for copy in last:
        copy.wait_recv()
    density = dens_slots[0]
    for k in range(1, orbs):
        density = density + dens_slots[k]
    dens_ref[...] = density * (4.0 / total_orbs)
    for copy in sent:
        copy.wait_send()


def solution(mesh):
    slabs, pens, orbs = mesh.shape["slab"], mesh.shape["pen"], mesh.shape["orb"]

    def on_device(
        orbitals, energies, frequency, local_potential, perturbation, projectors, profiles,
        couplings, atom_planes,
    ):
        count, planes, rows, width = orbitals.shape
        atoms = projectors.shape[0]
        total_orbs, group = count * orbs, slabs * pens
        vmem = pl.BlockSpec(memory_space=pltpu.VMEM)
        smem = pl.BlockSpec(memory_space=pltpu.SMEM)
        dma = pltpu.SemaphoreType.DMA
        response, density = pl.pallas_call(
            functools.partial(kernel, slabs, pens, orbs),
            out_shape=(
                jax.ShapeDtypeStruct((planes, rows, count, width), f32),
                jax.ShapeDtypeStruct((planes, rows, width), f32),
            ),
            in_specs=[vmem, vmem, smem, vmem, vmem, vmem, vmem, vmem, vmem],
            out_specs=(vmem, vmem),
            scratch_shapes=[
                pltpu.VMEM((orbs - 1, planes, rows, count, width), f32),
                pltpu.VMEM((2, orbs, rows, count, width), f32),
                pltpu.VMEM((2, rows, total_orbs, width), bf16),
                pltpu.VMEM((2, rows, total_orbs, width), bf16),
                pltpu.VMEM((2, rows, width), f32),
                pltpu.VMEM((2, rows, count, width), f32),
                pltpu.VMEM((planes, rows, total_orbs, width), bf16),
                pltpu.VMEM((planes, rows, total_orbs, width), bf16),
                pltpu.VMEM((planes, rows, atoms, width), bf16),
                pltpu.VMEM((planes, rows, atoms, width), bf16),
                pltpu.VMEM((planes + 2, rows + 2, count, width), f32),
                pltpu.VMEM((planes + 2, rows + 2, count, width), f32),
                pltpu.VMEM((planes + 2, rows + 2, count, width), f32),
                pltpu.VMEM((planes, rows, count, width), f32),
                pltpu.VMEM((orbs, planes, rows, width), f32),
                pltpu.VMEM((group, (total_orbs + count) // 2, 2 * total_orbs), f32),
                pltpu.VMEM((5, group, count, atoms), f32),
                dma((orbs - 1, 3)), dma((orbs - 1, 3)),
                dma((orbs + 2, 2)), dma((orbs + 2, 2)),
                dma((3, 4)), dma((3, 4)),
                dma((6, group - 1)), dma((6, group - 1)),
                dma((orbs - 1,)), dma((orbs - 1,)),
            ],
            compiler_params=pltpu.CompilerParams(collective_id=0, has_side_effects=True),
        )(
            jnp.transpose(orbitals, (1, 2, 0, 3)),
            energies[None, :],
            frequency,
            local_potential,
            perturbation,
            projectors,
            profiles.T,
            atom_planes[None, :],
            couplings[None, :],
        )
        return jnp.transpose(response, (2, 0, 1, 3)), density

    in_specs = (
        P(("parts", "orb"), "slab", "pen", None), P(("parts", "orb")), P("parts"),
        P("slab", "pen", None), P("slab", "pen", None), P(None, "pen", None), P(), P(), P(),
    )
    out_specs = (P(("parts", "orb"), "slab", "pen", None), P(("parts", "slab"), "pen", None))
    return jax.shard_map(
        on_device, mesh=mesh, in_specs=in_specs, out_specs=out_specs, check_vma=False
    )
```
